32 devices in a mesh: groups: 2 (over y), row: 16 (over z, x, core).
Axes of the slice: x: 2, y: 2, z: 4, core: 2. Of those that a mesh axis runs over, the one named last changes fastest.
Arguments:
- frames_in: bfloat16 [512, 6144], P(('groups', 'row')), parts along dimension 0, may hold values from -6 to 6
- clip_ids: int32 [512], P(('groups', 'row')), parts along dimension 0, may hold values from 0 to 15, as said below
- norm_gain: float32 [6144], replicated, may hold values from 0.1 to 1.9
- expand_weight: bfloat16 [6144, 24576], P(None, 'row'), may hold values from -0.078125 to 0.078125
- reduce_weight: bfloat16 [24576, 6144], P('row'), may hold values from -0.0390625 to 0.0390625
- conn_gain: float32 [6144], replicated, may hold values from 0.1 to 1.9
- conn_weight: bfloat16 [6144, 8192], P(None, 'row'), may hold values from -0.078125 to 0.078125
Outputs:
- visual_tokens: bfloat16 [32, 8192], P(('groups', 'row')), parts along dimension 0
The draws below stay inside these ranges and needn't reach their ends.
There are 2 independent parts, one for each index of `groups`. The reference program is written for one: setup_inputs(seed, part) draws one part's arguments, and reference() takes and returns one part's arrays. A program takes and returns all parts, laid end to end along the dimension named above; an argument that names none is the same for every part. Nothing has to cross between parts.
Inputs may be any that keep to these rules, and one draw needn't show every extreme that they name: `clip_ids`: every clip number is named by exactly 16 frame tokens, which may lie on any devices.
All inputs are finite; a program needn't handle non-finite values.
Results may differ from the reference program's by a relative error of at most 0.0058.
Values may be sent and summed in bfloat16 or wider, within the bound.
A program may use at most 384 MiB of HBM per device.

```python
import jax
import jax.numpy as jnp
from jax import lax

D = 6144
FF = 24576
E = 8192
FRAMES = 16
CLIPS = 16
TOKENS = 256


def draw_clip_ids(key, part):
    shuffled = jax.random.permutation(key, TOKENS)
    return (shuffled // FRAMES).astype(jnp.int32)


def shard_levels(rng, dims, shards, least, high):
    level, own = 1.0, jax.random.fold_in(rng, 6)
    for position, parts in shards:
        heights = jnp.exp(jax.random.uniform(jax.random.fold_in(own, position), (parts,), jnp.float32, least / len(shards), high / len(shards)))
        level = level * jnp.repeat(heights, dims[position] // parts).reshape([-1 if axis == position else 1 for axis in range(len(dims))])
    return level


def scatter_about(own_key, dims, width, limit, pieces=(), kind=jnp.bfloat16):
    values = width * jax.random.normal(own_key, dims, jnp.float32)
    if pieces:
        values = values * shard_levels(own_key, dims, pieces, -0.22, 0.18)
    return jnp.clip(values, -limit, limit).astype(kind)


def setup_inputs(seed: int = 0, part: int = 0) -> dict:
    keys = jax.random.split(jax.random.key(seed), 8)
    own_keys = jax.random.split(jax.random.fold_in(keys[7], part), 8)
    return {
        "frames_in": scatter_about(own_keys[0], (TOKENS, D), 1.0, 6.0, ((0, 16),)),
        "clip_ids": draw_clip_ids(jax.random.fold_in(jax.random.fold_in(keys[7], part), 71), part),
        "norm_gain": jnp.clip(1.0 + 0.18 * jax.random.normal(keys[2], (D,), jnp.float32), 0.1, 1.9),
        "expand_weight": scatter_about(keys[3], (D, FF), D ** -0.5, 0.078125, ((1, 16),)),
        "reduce_weight": scatter_about(keys[4], (FF, D), FF ** -0.5, 0.0390625, ((0, 16),)),
        "conn_gain": jnp.clip(1.0 + 0.18 * jax.random.normal(keys[5], (D,), jnp.float32), 0.1, 1.9),
        "conn_weight": scatter_about(keys[6], (D, E), D ** -0.5, 0.078125, ((1, 16),)),
    }


def layer_norm(values, gain_row):
    average = lax.optimization_barrier(jnp.mean(values, axis=-1, keepdims=True))
    centered = values - average
    variance = lax.optimization_barrier(jnp.mean(centered * centered, axis=-1, keepdims=True))
    return centered * lax.rsqrt(variance + 1e-06) * gain_row

def reference(frames_in, clip_ids, norm_gain, expand_weight, reduce_weight, conn_gain, conn_weight):
    normed = layer_norm(frames_in.astype(jnp.float32), norm_gain).astype(jnp.bfloat16)
    onehot = (clip_ids[:, None] == jnp.arange(CLIPS, dtype=jnp.int32)[None, :]).astype(jnp.float32)
    stacked = jnp.transpose(expand_weight.reshape(D, 8, FF // 8), (1, 0, 2))

    def pool_block(weight_block):
        pre_act = jnp.dot(normed, weight_block, preferred_element_type=jnp.float32)
        hidden = jax.nn.gelu(pre_act, approximate=False).astype(jnp.bfloat16)
        return jnp.dot(onehot.T, hidden.astype(jnp.float32), precision=lax.Precision.HIGHEST)
    pooled_blocks = lax.map(pool_block, stacked)
    summed = jnp.transpose(pooled_blocks, (1, 0, 2)).reshape(CLIPS, FF)
    pooled_hidden = (summed / FRAMES).astype(jnp.bfloat16)
    residual = jnp.dot(onehot.T, frames_in.astype(jnp.float32), precision=lax.Precision.HIGHEST) / FRAMES
    pooled = residual + jnp.dot(pooled_hidden, reduce_weight, preferred_element_type=jnp.float32)
    connected = layer_norm(pooled, conn_gain).astype(jnp.bfloat16)
    return jnp.dot(connected, conn_weight, preferred_element_type=jnp.float32).astype(jnp.bfloat16)
```

```python
import jax
import jax.numpy as jnp
from jax import lax
from jax.sharding import PartitionSpec as P

FRAMES = 16


epsilon = 1e-06


def layer_norm(values, gain_row):
    average = jnp.mean(values, axis=-1, keepdims=True)
    centered = values - average
    variance = jnp.mean(centered * centered, axis=-1, keepdims=True)
    return centered * lax.rsqrt(variance + epsilon) * gain_row


def clip_onehot(clip_list, clip_count):
    return (clip_list[:, None] == jnp.arange(clip_count, dtype=jnp.int32)[None, :]).astype(
        jnp.bfloat16
    )


def pool_rows(onehot, values):
    return lax.dot_general(
        onehot, values, (((0,), (0,)), ((), ())), preferred_element_type=jnp.float32
    )


def hidden_pool(row_block, clip_list, weight_block, clip_count):
    pre_act = jnp.dot(row_block, weight_block, preferred_element_type=jnp.float32)
    hidden = jax.nn.gelu(pre_act, approximate=False).astype(jnp.bfloat16)
    return pool_rows(clip_onehot(clip_list, clip_count), hidden)


def local(frames_in, clip_ids, norm_gain, expand_weight, reduce_weight, conn_gain, conn_weight):
    devices_row = lax.axis_size("row")
    tok_local = frames_in.shape[0]
    clip_count = devices_row * (tok_local // FRAMES)
    normed = layer_norm(frames_in.astype(jnp.float32), norm_gain).astype(jnp.bfloat16)
    residual = pool_rows(clip_onehot(clip_ids, clip_count), frames_in) / FRAMES
    every_row = lax.all_gather(normed, "row", axis=0, tiled=True)
    every_id = lax.all_gather(clip_ids, "row", axis=0, tiled=True)
    summed = hidden_pool(every_row, every_id, expand_weight, clip_count)
    pooled_hidden = (summed / FRAMES).astype(jnp.bfloat16)
    partial_value = residual + jnp.dot(
        pooled_hidden, reduce_weight, preferred_element_type=jnp.float32
    )
    owned_rows = lax.psum_scatter(partial_value, "row", scatter_dimension=0, tiled=True)
    connected = layer_norm(owned_rows, conn_gain).astype(jnp.bfloat16)
    every_clip = lax.all_gather(connected, "row", axis=0, tiled=True)
    projected = jnp.dot(every_clip, conn_weight, preferred_element_type=jnp.float32).astype(
        jnp.bfloat16
    )
    return lax.all_to_all(projected, "row", split_axis=0, concat_axis=1, tiled=True)


def solution(mesh):
    in_specs = (
        P(("groups", "row"), None),
        P(("groups", "row")),
        P(),
        P(None, "row"),
        P("row", None),
        P(),
        P(None, "row"),
    )
    out_specs = P(("groups", "row"), None)
    return jax.shard_map(local, mesh=mesh, in_specs=in_specs, out_specs=out_specs, check_vma=False)
```

```python
import functools

import jax
import jax.numpy as jnp
from jax import lax
from jax.experimental import pallas as pl
from jax.experimental.pallas import tpu as pltpu
from jax.sharding import PartitionSpec as P

FRAMES = 16
LANES = 128
MESH = pl.DeviceIdType.MESH
epsilon = 1e-06


def layer_norm(values, gain_row):
    average = jnp.mean(values, axis=-1, keepdims=True)
    centered = values - average
    variance = jnp.mean(centered * centered, axis=-1, keepdims=True)
    return centered * lax.rsqrt(variance + epsilon) * gain_row


def clip_onehot(clip_list, clip_count):
    return (clip_list[:, None] == jnp.arange(clip_count, dtype=jnp.int32)[None, :]).astype(
        jnp.bfloat16
    )


def pool_rows(onehot, values):
    return lax.dot_general(
        onehot, values, (((0,), (0,)), ((), ())), preferred_element_type=jnp.float32
    )


def hidden_pool(row_block, clip_list, weight_block, clip_count):
    pre_act = jnp.dot(row_block, weight_block, preferred_element_type=jnp.float32)
    hidden = jax.nn.gelu(pre_act, approximate=False).astype(jnp.bfloat16)
    return pool_rows(clip_onehot(clip_list, clip_count), hidden)


def plain(frames_in, clip_ids, norm_gain, expand_weight, reduce_weight, conn_gain, conn_weight):
    devices_row = lax.axis_size("row")
    tok_local = frames_in.shape[0]
    clip_count = devices_row * (tok_local // FRAMES)
    normed = layer_norm(frames_in.astype(jnp.float32), norm_gain).astype(jnp.bfloat16)
    residual = pool_rows(clip_onehot(clip_ids, clip_count), frames_in) / FRAMES
    every_row = lax.all_gather(normed, "row", axis=0, tiled=True)
    every_id = lax.all_gather(clip_ids, "row", axis=0, tiled=True)
    summed = hidden_pool(every_row, every_id, expand_weight, clip_count)
    pooled_hidden = (summed / FRAMES).astype(jnp.bfloat16)
    partial_value = residual + jnp.dot(
        pooled_hidden, reduce_weight, preferred_element_type=jnp.float32
    )
    owned_rows = lax.psum_scatter(partial_value, "row", scatter_dimension=0, tiled=True)
    connected = layer_norm(owned_rows, conn_gain).astype(jnp.bfloat16)
    every_clip = lax.all_gather(connected, "row", axis=0, tiled=True)
    projected = jnp.dot(every_clip, conn_weight, preferred_element_type=jnp.float32).astype(
        jnp.bfloat16
    )
    return lax.all_to_all(projected, "row", split_axis=0, concat_axis=1, tiled=True)


def copy_block(buf, block, send, slot, recv, to):
    return pltpu.make_async_remote_copy(
        src_ref=buf.at[block],
        dst_ref=buf.at[block],
        send_sem=send.at[slot],
        recv_sem=recv.at[block],
        device_id={"row": to},
        device_id_type=MESH,
    )


def spread_blocks(buf, send, recv, n, me):
    core, chip = me % 2, me // 2
    x, z, depth = chip % 2, chip // 2, n // 4
    partner = chip * 2 + (1 - core)
    beside = (z * 2 + 1 - x) * 2 + core
    started = []

    def go(block, to):
        copy = copy_block(buf, block, send, len(started), recv, to)
        copy.start()
        started.append(copy)

    def arrive(block):
        copy_block(buf, block, send, 0, recv, partner).wait_recv()

    go(me, beside)
    for step in range(1, depth):
        go(me, (((z + step) % depth) * 2 + x) * 2 + core)
    go(me, partner)
    arrive(beside)
    go(beside, partner)
    for step in range(1, depth):
        block = (((z + depth - step) % depth) * 2 + x) * 2 + core
        arrive(block)
        go(block, beside)
        go(block, partner)
    for step in range(1, depth):
        block = (((z + depth - step) % depth) * 2 + 1 - x) * 2 + core
        arrive(block)
        go(block, partner)
    for other in range(n // 2):
        arrive(other * 2 + 1 - core)
    return started


def kernel(
    n, frames_ref, idcol_ref, idrow_ref, ngain_ref, w1_hbm, w2_hbm, cgain_ref, w3_hbm, out_ref,
    rows, w1, w2, w3, onehot_t, ph, part, landed, red, conn, proj, arrived,
    w_sem, g_send, g_recv, r_send, r_recv, a_send, a_recv, o_send, o_recv,
):
    me = lax.axis_index("row")
    tok, dim = frames_ref.shape
    clips = ph.shape[0]
    width = w1.shape[1]
    bw = part.shape[2]
    ew = w3.shape[1]
    barrier = pltpu.get_barrier_semaphore()
    for step in range(1, n):
        pl.semaphore_signal(
            barrier, inc=1, device_id={"row": (me + step) % n}, device_id_type=MESH
        )
    loads = []
    for index, (src, dst) in enumerate(((w1_hbm, w1), (w2_hbm, w2), (w3_hbm, w3))):
        tall = src.shape[0] // 4
        group = []
        for piece in range(4):
            span = pl.ds(piece * tall, tall)
            load = pltpu.make_async_copy(src.at[span], dst.at[span], w_sem.at[index, piece])
            load.start()
            group.append(load)
        loads.append(group)

    normed = layer_norm(frames_ref[...].astype(jnp.float32), ngain_ref[...])
    rows[me, :, 0:dim] = normed.astype(jnp.bfloat16)
    rows[me, :, dim : dim + LANES] = idcol_ref[...].astype(jnp.float32).astype(jnp.bfloat16)
    pl.semaphore_wait(barrier, n - 1)
    sent = spread_blocks(rows, g_send, g_recv, n, me)

    every_id = rows[:, :, dim : dim + LANES].reshape(n * tok, LANES).astype(jnp.float32)
    lane = lax.broadcasted_iota(jnp.int32, (n * tok, LANES), 1).astype(jnp.float32)
    onehot = jnp.where(every_id == lane, 1.0, 0.0)
    onehot_t[...] = jnp.transpose(onehot)[0:clips].astype(jnp.bfloat16)
    for load in loads[0]:
        load.wait()
    cw = 256

    @pl.loop(0, width // cw)
    def _(step):
        cols = pl.ds(pl.multiple_of(step * cw, cw), cw)
        pre_act = jnp.dot(
            rows[:, :, 0:dim].reshape(n * tok, dim), w1[:, cols], preferred_element_type=jnp.float32
        )
        hidden = 0.5 * pre_act * (1.0 + lax.erf(pre_act * 0.7071067811865476))
        summed = jnp.dot(
            onehot_t[...], hidden.astype(jnp.bfloat16), preferred_element_type=jnp.float32
        )
        ph[:, cols] = (summed / FRAMES).astype(jnp.bfloat16)

    for copy in sent:
        copy.wait_send()
    for load in loads[1]:
        load.wait()
    own_hot = jnp.where(
        lax.broadcasted_iota(jnp.int32, (clips, tok), 0) == idrow_ref[...], 1.0, 0.0
    ).astype(jnp.bfloat16)

    def term(owner):
        cols = pl.ds(pl.multiple_of(owner * bw, LANES), bw)
        residual = jnp.dot(own_hot, frames_ref[:, cols], preferred_element_type=jnp.float32)
        return residual / FRAMES + jnp.dot(
            ph[...], w2[:, cols], preferred_element_type=jnp.float32
        )

    def give(step):
        owner = (me + 1 + step) % n
        return pltpu.make_async_remote_copy(
            src_ref=part.at[owner],
            dst_ref=landed.at[me],
            send_sem=r_send.at[step],
            recv_sem=r_recv.at[me],
            device_id={"row": owner},
            device_id_type=MESH,
        )

    @pl.loop(0, n - 1)
    def _(step):
        owner = (me + 1 + step) % n
        part[owner] = term(owner)

        @pl.when(step > 0)
        def _():
            give(step - 1).start()

    total = term(me)
    give(n - 2).start()
    for step in range(1, n):
        source = (me + n - step) % n
        pltpu.make_async_remote_copy(
            src_ref=part.at[source],
            dst_ref=landed.at[source],
            send_sem=r_send.at[0],
            recv_sem=r_recv.at[source],
            device_id={"row": source},
            device_id_type=MESH,
        ).wait_recv()
        total = total + landed[source]
    red[me] = total
    for step in range(n - 1):
        give(step).wait_send()
    sent = spread_blocks(red, a_send, a_recv, n, me)

    pooled = red[...]
    average = jnp.sum(jnp.sum(pooled, axis=0), axis=-1, keepdims=True) / dim
    centered = pooled - average[None]
    variance = jnp.sum(jnp.sum(centered * centered, axis=0), axis=-1, keepdims=True) / dim
    scale = lax.rsqrt(variance + epsilon)
    for block in range(n):
        cols = slice(block * bw, (block + 1) * bw)
        conn[:, cols] = ((red[block] - average) * scale * cgain_ref[:, cols]).astype(jnp.bfloat16)
    for load in loads[2]:
        load.wait()
    projected = jnp.dot(conn[...], w3[...], preferred_element_type=jnp.float32)
    for clip in range(clips):
        proj[clip] = projected[clip : clip + 1]
    arrived[pl.ds(me, 1)] = proj[pl.ds(me, 1)]
    for copy in sent:
        copy.wait_send()
    outs = []
    for step in range(1, n):
        owner = (me + step) % n
        copy = pltpu.make_async_remote_copy(
            src_ref=proj.at[owner],
            dst_ref=arrived.at[me],
            send_sem=o_send.at[step],
            recv_sem=o_recv.at[me],
            device_id={"row": owner},
            device_id_type=MESH,
        )
        copy.start()
        outs.append(copy)
    for step in range(1, n):
        source = (me + n - step) % n
        pltpu.make_async_remote_copy(
            src_ref=proj.at[source],
            dst_ref=arrived.at[source],
            send_sem=o_send.at[0],
            recv_sem=o_recv.at[source],
            device_id={"row": source},
            device_id_type=MESH,
        ).wait_recv()
    for block in range(n):
        out_ref[:, block * ew : (block + 1) * ew] = arrived[block].astype(jnp.bfloat16)
    for copy in outs:
        copy.wait_send()


def fused(frames_in, clip_ids, norm_gain, expand_weight, reduce_weight, conn_gain, conn_weight):
    n = lax.axis_size("row")
    tok, dim = frames_in.shape
    width, ew = expand_weight.shape[1], conn_weight.shape[1]
    bw = dim // n
    vmem, hbm = pl.BlockSpec(memory_space=pltpu.VMEM), pl.BlockSpec(memory_space=pl.ANY)
    dma = pltpu.SemaphoreType.DMA
    f32, bf16 = jnp.float32, jnp.bfloat16
    return pl.pallas_call(
        functools.partial(kernel, n),
        name="vision_block",
        out_shape=jax.ShapeDtypeStruct((1, n * ew), bf16),
        in_specs=[vmem, vmem, vmem, vmem, hbm, hbm, vmem, hbm],
        out_specs=vmem,
        scratch_shapes=[
            pltpu.VMEM((n, tok, dim + LANES), bf16),
            pltpu.VMEM((dim, width), bf16),
            pltpu.VMEM((width, dim), bf16),
            pltpu.VMEM((dim, ew), bf16),
            pltpu.VMEM((n, n * tok), bf16),
            pltpu.VMEM((n, width), bf16),
            pltpu.VMEM((n, n, bw), f32),
            pltpu.VMEM((n, n, bw), f32),
            pltpu.VMEM((n, n, bw), f32),
            pltpu.VMEM((n, dim), bf16),
            pltpu.VMEM((n, 1, ew), f32),
            pltpu.VMEM((n, 1, ew), f32),
            dma((3, 4)),
            dma((n,)), dma((n,)), dma((n,)), dma((n,)),
            dma((n,)), dma((n,)), dma((n,)), dma((n,)),
        ],
        compiler_params=pltpu.CompilerParams(
            collective_id=0, has_side_effects=True, vmem_limit_bytes=60 * 1024 * 1024
        ),
    )(
        frames_in,
        jnp.broadcast_to(clip_ids[:, None], (tok, LANES)),
        clip_ids[None, :],
        norm_gain[None, :],
        expand_weight,
        reduce_weight,
        conn_gain[None, :],
        conn_weight,
    )


def local(frames_in, clip_ids, norm_gain, expand_weight, reduce_weight, conn_gain, conn_weight):
    n = lax.axis_size("row")
    tok, dim = frames_in.shape
    width, ew = expand_weight.shape[1], conn_weight.shape[1]
    fits = tok == FRAMES and n % 16 == 0 and n <= LANES and (n * tok) % LANES == 0
    even = dim % (n * LANES) == 0 and width % 256 == 0 and ew % LANES == 0
    form = fused if fits and even else plain
    return form(
        frames_in, clip_ids, norm_gain, expand_weight, reduce_weight, conn_gain, conn_weight
    )


def solution(mesh):
    in_specs = (
        P(("groups", "row"), None),
        P(("groups", "row")),
        P(),
        P(None, "row"),
        P("row", None),
        P(),
        P(None, "row"),
    )
    out_specs = P(("groups", "row"), None)
    return jax.shard_map(local, mesh=mesh, in_specs=in_specs, out_specs=out_specs, check_vma=False)
```

```python
import functools

import jax
import jax.numpy as jnp
from jax import lax
from jax.experimental import pallas as pl
from jax.experimental.pallas import tpu as pltpu
from jax.sharding import PartitionSpec as P

FRAMES = 16
LANES = 128
PIECES = 2
MESH = pl.DeviceIdType.MESH
epsilon = 1e-06


def layer_norm(values, gain_row):
    average = jnp.mean(values, axis=-1, keepdims=True)
    centered = values - average
    variance = jnp.mean(centered * centered, axis=-1, keepdims=True)
    return centered * lax.rsqrt(variance + epsilon) * gain_row


def clip_onehot(clip_list, clip_count):
    return (clip_list[:, None] == jnp.arange(clip_count, dtype=jnp.int32)[None, :]).astype(
        jnp.bfloat16
    )


def pool_rows(onehot, values):
    return lax.dot_general(
        onehot, values, (((0,), (0,)), ((), ())), preferred_element_type=jnp.float32
    )


def hidden_pool(row_block, clip_list, weight_block, clip_count):
    pre_act = jnp.dot(row_block, weight_block, preferred_element_type=jnp.float32)
    hidden = jax.nn.gelu(pre_act, approximate=False).astype(jnp.bfloat16)
    return pool_rows(clip_onehot(clip_list, clip_count), hidden)


def plain(frames_in, clip_ids, norm_gain, expand_weight, reduce_weight, conn_gain, conn_weight):
    devices_row = lax.axis_size("row")
    tok_local = frames_in.shape[0]
    clip_count = devices_row * (tok_local // FRAMES)
    normed = layer_norm(frames_in.astype(jnp.float32), norm_gain).astype(jnp.bfloat16)
    residual = pool_rows(clip_onehot(clip_ids, clip_count), frames_in) / FRAMES
    every_row = lax.all_gather(normed, "row", axis=0, tiled=True)
    every_id = lax.all_gather(clip_ids, "row", axis=0, tiled=True)
    summed = hidden_pool(every_row, every_id, expand_weight, clip_count)
    pooled_hidden = (summed / FRAMES).astype(jnp.bfloat16)
    partial_value = residual + jnp.dot(
        pooled_hidden, reduce_weight, preferred_element_type=jnp.float32
    )
    owned_rows = lax.psum_scatter(partial_value, "row", scatter_dimension=0, tiled=True)
    connected = layer_norm(owned_rows, conn_gain).astype(jnp.bfloat16)
    every_clip = lax.all_gather(connected, "row", axis=0, tiled=True)
    projected = jnp.dot(every_clip, conn_weight, preferred_element_type=jnp.float32).astype(
        jnp.bfloat16
    )
    return lax.all_to_all(projected, "row", split_axis=0, concat_axis=1, tiled=True)


def copy_block(buf, block, send, slot, recv, to):
    return pltpu.make_async_remote_copy(
        src_ref=buf.at[block],
        dst_ref=buf.at[block],
        send_sem=send.at[slot],
        recv_sem=recv.at[block],
        device_id={"row": to},
        device_id_type=MESH,
    )


def spread_blocks(buf, send, recv, n, me):
    core, chip = me % 2, me // 2
    x, z, depth = chip % 2, chip // 2, n // 4
    partner = chip * 2 + (1 - core)
    beside = (z * 2 + 1 - x) * 2 + core
    started = []

    def go(block, to):
        copy = copy_block(buf, block, send, len(started), recv, to)
        copy.start()
        started.append(copy)

    def arrive(block):
        copy_block(buf, block, send, 0, recv, partner).wait_recv()

    go(me, beside)
    for step in range(1, depth):
        go(me, (((z + step) % depth) * 2 + x) * 2 + core)
    go(me, partner)
    arrive(beside)
    go(beside, partner)
    for step in range(1, depth):
        block = (((z + depth - step) % depth) * 2 + x) * 2 + core
        arrive(block)
        go(block, beside)
        go(block, partner)
    for step in range(1, depth):
        block = (((z + depth - step) % depth) * 2 + 1 - x) * 2 + core
        arrive(block)
        go(block, partner)
    for other in range(n // 2):
        arrive(other * 2 + 1 - core)
    return started


def kernel(
    n, frames_ref, idrow_ref, ngain_ref, w1_hbm, w2_hbm, cgain_ref, w3_hbm, out_ref,
    rows, acc, w1, w2, w3, onehot_t, ph, part, landed, red, conn, proj, arrived,
    w_sem, g_send, g_recv, r_send, r_recv, a_send, a_recv, o_send, o_recv,
):
    me = lax.axis_index("row")
    tok, dim = frames_ref.shape
    clips = ph.shape[0]
    width = w1.shape[1]
    bw = part.shape[2]
    ew = w3.shape[1]
    barrier = pltpu.get_barrier_semaphore()
    for step in range(1, n):
        pl.semaphore_signal(
            barrier, inc=1, device_id={"row": (me + step) % n}, device_id_type=MESH
        )
    loads = []
    for index, (src, dst) in enumerate(((w1_hbm, w1), (w2_hbm, w2), (w3_hbm, w3))):
        tall = src.shape[0] // PIECES
        group = []
        for piece in range(PIECES):
            span = pl.ds(piece * tall, tall)
            load = pltpu.make_async_copy(src.at[span], dst.at[span], w_sem.at[index, piece])
            load.start()
            group.append(load)
        loads.append(group)

    normed = layer_norm(frames_ref[...].astype(jnp.float32), ngain_ref[...])
    rows[me, :, 0:dim] = normed.astype(jnp.bfloat16)
    diagonal = lax.broadcasted_iota(jnp.int32, (tok, tok), 0) == lax.broadcasted_iota(
        jnp.int32, (tok, tok), 1
    )
    own_ids = jnp.where(diagonal, idrow_ref[...].astype(jnp.float32), 0.0)
    id_column = jnp.sum(own_ids, axis=1, keepdims=True)
    rows[me, :, dim : dim + LANES] = jnp.broadcast_to(id_column, (tok, LANES)).astype(jnp.bfloat16)
    pl.semaphore_wait(barrier, n - 1)

    core, chip = me % 2, me // 2
    x, z, depth = chip % 2, chip // 2, n // 4
    partner = chip * 2 + (1 - core)
    beside = (z * 2 + 1 - x) * 2 + core
    deep = dim // PIECES
    sent = []

    def piece_copy(block, piece, slot, to):
        end = dim + LANES if piece == PIECES - 1 else (piece + 1) * deep
        spot = rows.at[block, :, piece * deep : end]
        return pltpu.make_async_remote_copy(
            src_ref=spot,
            dst_ref=spot,
            send_sem=g_send.at[slot],
            recv_sem=g_recv.at[block, piece],
            device_id={"row": to},
            device_id_type=MESH,
        )

    def go(block, piece, to, when=True):
        copy = piece_copy(block, piece, len(sent), to)
        sent.append((copy, when))
        if when is True:
            copy.start()
        else:
            pl.when(when)(copy.start)

    def arrive(block, piece):
        piece_copy(block, piece, 0, partner).wait_recv()

    hops = [(step, way) for step in range(1, depth) for way in (1, -1)]

    def inside(level):
        return jnp.logical_and(level >= 0, level < depth)

    def rail(level, side):
        return (level * 2 + side) * 2 + core

    def finish(piece):
        for step, way in hops:
            origin = z - way * step
            block = rail(origin, 1 - x)
            pl.when(inside(origin))(functools.partial(arrive, block, piece))
            go(block, piece, partner, inside(origin))
        for other in range(n // 2):
            arrive(other * 2 + 1 - core, piece)
        loads[0][piece].wait()

    cw = 256

    def product(piece, cols):
        span = slice(piece * deep, (piece + 1) * deep)
        return jnp.dot(
            rows[:, :, span].reshape(n * tok, deep), w1[span, cols], preferred_element_type=jnp.float32
        )

    for piece in range(PIECES):
        go(me, piece, beside)
        for way in (1, -1):
            go(me, piece, rail(z + way, x), inside(z + way))
        go(me, piece, partner)
    for piece in range(PIECES):
        arrive(beside, piece)
        go(beside, piece, partner)
        for step, way in hops:
            origin = z - way * step
            block = rail(origin, x)
            here = inside(origin)
            pl.when(here)(functools.partial(arrive, block, piece))
            if step < depth - 1:
                go(block, piece, rail(z + way, x), jnp.logical_and(here, inside(z + way)))
            go(block, piece, beside, here)
            go(block, piece, partner, here)
        if piece > 0:
            finish(piece - 1)

            @pl.loop(0, width // cw)
            def _(step):
                cols = pl.ds(pl.multiple_of(step * cw, cw), cw)
                if piece == 1:
                    acc[:, cols] = product(0, cols)
                else:
                    acc[:, cols] += product(piece - 1, cols)

    finish(PIECES - 1)
    every_id = rows[:, :, dim : dim + LANES].reshape(n * tok, LANES).astype(jnp.float32)
    lane = lax.broadcasted_iota(jnp.int32, (n * tok, LANES), 1).astype(jnp.float32)
    onehot = jnp.where(every_id == lane, 1.0, 0.0)
    onehot_t[...] = jnp.transpose(onehot)[0:clips].astype(jnp.bfloat16)

    @pl.loop(0, width // cw)
    def _(step):
        cols = pl.ds(pl.multiple_of(step * cw, cw), cw)
        pre_act = acc[:, cols] + product(PIECES - 1, cols)
        hidden = 0.5 * pre_act * (1.0 + lax.erf(pre_act * 0.7071067811865476))
        summed = jnp.dot(
            onehot_t[...], hidden.astype(jnp.bfloat16), preferred_element_type=jnp.float32
        )
        ph[:, cols] = (summed / FRAMES).astype(jnp.bfloat16)

    for copy, when in sent:
        if when is True:
            copy.wait_send()
        else:
            pl.when(when)(copy.wait_send)
    for load in loads[1]:
        load.wait()
    own_hot = jnp.where(
        lax.broadcasted_iota(jnp.int32, (clips, tok), 0) == idrow_ref[...], 1.0, 0.0
    ).astype(jnp.bfloat16)

    def term(owner):
        cols = pl.ds(pl.multiple_of(owner * bw, LANES), bw)
        residual = jnp.dot(own_hot, frames_ref[:, cols], preferred_element_type=jnp.float32)
        return residual / FRAMES + jnp.dot(
            ph[...], w2[:, cols], preferred_element_type=jnp.float32
        )

    def give(step):
        owner = (me + 1 + step) % n
        return pltpu.make_async_remote_copy(
            src_ref=part.at[owner],
            dst_ref=landed.at[me],
            send_sem=r_send.at[step],
            recv_sem=r_recv.at[me],
            device_id={"row": owner},
            device_id_type=MESH,
        )

    @pl.loop(0, n - 1)
    def _(step):
        owner = (me + 1 + step) % n
        part[owner] = term(owner)

        @pl.when(step > 0)
        def _():
            give(step - 1).start()

    total = term(me)
    give(n - 2).start()
    for step in range(1, n):
        source = (me + n - step) % n
        pltpu.make_async_remote_copy(
            src_ref=part.at[source],
            dst_ref=landed.at[source],
            send_sem=r_send.at[0],
            recv_sem=r_recv.at[source],
            device_id={"row": source},
            device_id_type=MESH,
        ).wait_recv()
        total = total + landed[source]
    red[me] = total
    for step in range(n - 1):
        give(step).wait_send()
    sent = spread_blocks(red, a_send, a_recv, n, me)

    pooled = red[...]
    average = jnp.sum(jnp.sum(pooled, axis=0), axis=-1, keepdims=True) / dim
    centered = pooled - average[None]
    variance = jnp.sum(jnp.sum(centered * centered, axis=0), axis=-1, keepdims=True) / dim
    scale = lax.rsqrt(variance + epsilon)
    for block in range(n):
        cols = slice(block * bw, (block + 1) * bw)
        conn[:, cols] = ((red[block] - average) * scale * cgain_ref[:, cols]).astype(jnp.bfloat16)
    for load in loads[2]:
        load.wait()
    projected = jnp.dot(conn[...], w3[...], preferred_element_type=jnp.float32)
    for clip in range(clips):
        proj[clip] = projected[clip : clip + 1]
    arrived[pl.ds(me, 1)] = proj[pl.ds(me, 1)]
    for copy in sent:
        copy.wait_send()
    outs = []
    for step in range(1, n):
        owner = (me + step) % n
        copy = pltpu.make_async_remote_copy(
            src_ref=proj.at[owner],
            dst_ref=arrived.at[me],
            send_sem=o_send.at[step],
            recv_sem=o_recv.at[me],
            device_id={"row": owner},
            device_id_type=MESH,
        )
        copy.start()
        outs.append(copy)
    for step in range(1, n):
        source = (me + n - step) % n
        pltpu.make_async_remote_copy(
            src_ref=proj.at[source],
            dst_ref=arrived.at[source],
            send_sem=o_send.at[0],
            recv_sem=o_recv.at[source],
            device_id={"row": source},
            device_id_type=MESH,
        ).wait_recv()
    for block in range(n):
        out_ref[:, block * ew : (block + 1) * ew] = arrived[block].astype(jnp.bfloat16)
    for copy in outs:
        copy.wait_send()


def fused(frames_in, clip_ids, norm_gain, expand_weight, reduce_weight, conn_gain, conn_weight):
    n = lax.axis_size("row")
    tok, dim = frames_in.shape
    width, ew = expand_weight.shape[1], conn_weight.shape[1]
    bw = dim // n
    vmem, hbm = pl.BlockSpec(memory_space=pltpu.VMEM), pl.BlockSpec(memory_space=pl.ANY)
    dma = pltpu.SemaphoreType.DMA
    f32, bf16 = jnp.float32, jnp.bfloat16
    return pl.pallas_call(
        functools.partial(kernel, n),
        name="vision_block",
        out_shape=jax.ShapeDtypeStruct((1, n * ew), bf16),
        in_specs=[vmem, vmem, vmem, hbm, hbm, vmem, hbm],
        out_specs=vmem,
        scratch_shapes=[
            pltpu.VMEM((n, tok, dim + LANES), bf16),
            pltpu.VMEM((n * tok, width), f32),
            pltpu.VMEM((dim, width), bf16),
            pltpu.VMEM((width, dim), bf16),
            pltpu.VMEM((dim, ew), bf16),
            pltpu.VMEM((n, n * tok), bf16),
            pltpu.VMEM((n, width), bf16),
            pltpu.VMEM((n, n, bw), f32),
            pltpu.VMEM((n, n, bw), f32),
            pltpu.VMEM((n, n, bw), f32),
            pltpu.VMEM((n, dim), bf16),
            pltpu.VMEM((n, 1, ew), f32),
            pltpu.VMEM((n, 1, ew), f32),
            dma((3, PIECES)),
            dma((2 * n * PIECES,)), dma((n, PIECES)), dma((n,)), dma((n,)),
            dma((n,)), dma((n,)), dma((n,)), dma((n,)),
        ],
        compiler_params=pltpu.CompilerParams(
            collective_id=0, has_side_effects=True, vmem_limit_bytes=60 * 1024 * 1024
        ),
    )(
        frames_in,
        clip_ids[None, :],
        norm_gain[None, :],
        expand_weight,
        reduce_weight,
        conn_gain[None, :],
        conn_weight,
    )


def local(frames_in, clip_ids, norm_gain, expand_weight, reduce_weight, conn_gain, conn_weight):
    n = lax.axis_size("row")
    tok, dim = frames_in.shape
    width, ew = expand_weight.shape[1], conn_weight.shape[1]
    fits = tok == FRAMES and n % 16 == 0 and n <= LANES and (n * tok) % LANES == 0
    even = dim % (n * LANES) == 0 and width % 256 == 0 and ew % LANES == 0
    form = fused if fits and even else plain
    return form(
        frames_in, clip_ids, norm_gain, expand_weight, reduce_weight, conn_gain, conn_weight
    )


def solution(mesh):
    in_specs = (
        P(("groups", "row"), None),
        P(("groups", "row")),
        P(),
        P(None, "row"),
        P("row", None),
        P(),
        P(None, "row"),
    )
    out_specs = P(("groups", "row"), None)
    return jax.shard_map(local, mesh=mesh, in_specs=in_specs, out_specs=out_specs, check_vma=False)
```

```python
import functools

import jax
import jax.numpy as jnp
from jax import lax
from jax.experimental import pallas as pl
from jax.experimental.pallas import tpu as pltpu
from jax.sharding import PartitionSpec as P

FRAMES = 16
LANES = 128
PIECES = 2
MESH = pl.DeviceIdType.MESH
epsilon = 1e-06


def layer_norm(values, gain_row):
    average = jnp.mean(values, axis=-1, keepdims=True)
    centered = values - average
    variance = jnp.mean(centered * centered, axis=-1, keepdims=True)
    return centered * lax.rsqrt(variance + epsilon) * gain_row


def clip_onehot(clip_list, clip_count):
    return (clip_list[:, None] == jnp.arange(clip_count, dtype=jnp.int32)[None, :]).astype(
        jnp.bfloat16
    )


def pool_rows(onehot, values):
    return lax.dot_general(
        onehot, values, (((0,), (0,)), ((), ())), preferred_element_type=jnp.float32
    )


def hidden_pool(row_block, clip_list, weight_block, clip_count):
    pre_act = jnp.dot(row_block, weight_block, preferred_element_type=jnp.float32)
    hidden = jax.nn.gelu(pre_act, approximate=False).astype(jnp.bfloat16)
    return pool_rows(clip_onehot(clip_list, clip_count), hidden)


def plain(frames_in, clip_ids, norm_gain, expand_weight, reduce_weight, conn_gain, conn_weight):
    devices_row = lax.axis_size("row")
    tok_local = frames_in.shape[0]
    clip_count = devices_row * (tok_local // FRAMES)
    normed = layer_norm(frames_in.astype(jnp.float32), norm_gain).astype(jnp.bfloat16)
    residual = pool_rows(clip_onehot(clip_ids, clip_count), frames_in) / FRAMES
    every_row = lax.all_gather(normed, "row", axis=0, tiled=True)
    every_id = lax.all_gather(clip_ids, "row", axis=0, tiled=True)
    summed = hidden_pool(every_row, every_id, expand_weight, clip_count)
    pooled_hidden = (summed / FRAMES).astype(jnp.bfloat16)
    partial_value = residual + jnp.dot(
        pooled_hidden, reduce_weight, preferred_element_type=jnp.float32
    )
    owned_rows = lax.psum_scatter(partial_value, "row", scatter_dimension=0, tiled=True)
    connected = layer_norm(owned_rows, conn_gain).astype(jnp.bfloat16)
    every_clip = lax.all_gather(connected, "row", axis=0, tiled=True)
    projected = jnp.dot(every_clip, conn_weight, preferred_element_type=jnp.float32).astype(
        jnp.bfloat16
    )
    return lax.all_to_all(projected, "row", split_axis=0, concat_axis=1, tiled=True)


def copy_block(buf, block, send, slot, recv, to):
    return pltpu.make_async_remote_copy(
        src_ref=buf.at[block],
        dst_ref=buf.at[block],
        send_sem=send.at[slot],
        recv_sem=recv.at[block],
        device_id={"row": to},
        device_id_type=MESH,
    )


def spread_blocks(buf, send, recv, n, me):
    core, chip = me % 2, me // 2
    x, z, depth = chip % 2, chip // 2, n // 4
    partner = chip * 2 + (1 - core)
    beside = (z * 2 + 1 - x) * 2 + core
    started = []

    def go(block, to):
        copy = copy_block(buf, block, send, len(started), recv, to)
        copy.start()
        started.append(copy)

    def arrive(block):
        copy_block(buf, block, send, 0, recv, partner).wait_recv()

    go(me, beside)
    for step in range(1, depth):
        go(me, (((z + step) % depth) * 2 + x) * 2 + core)
    go(me, partner)
    arrive(beside)
    go(beside, partner)
    for step in range(1, depth):
        block = (((z + depth - step) % depth) * 2 + x) * 2 + core
        arrive(block)
        go(block, beside)
        go(block, partner)
    for step in range(1, depth):
        block = (((z + depth - step) % depth) * 2 + 1 - x) * 2 + core
        arrive(block)
        go(block, partner)
    for other in range(n // 2):
        arrive(other * 2 + 1 - core)
    return started


def kernel(
    n, frames_ref, idrow_ref, ngain_ref, w1_hbm, w2_hbm, cgain_ref, w3_hbm, out_ref,
    rows, acc, w1, w2, w3, onehot_t, ph, part, landed, red, conn, proj, arrived,
    w_sem, g_send, g_recv, r_send, r_recv, a_send, a_recv, o_send, o_recv,
):
    me = lax.axis_index("row")
    tok, dim = frames_ref.shape
    clips = ph.shape[0]
    width = w1.shape[1]
    bw = part.shape[2]
    ew = w3.shape[1]
    barrier = pltpu.get_barrier_semaphore()
    for step in range(1, n):
        pl.semaphore_signal(
            barrier, inc=1, device_id={"row": (me + step) % n}, device_id_type=MESH
        )
    loads = []
    for index, (src, dst) in enumerate(((w1_hbm, w1), (w2_hbm, w2), (w3_hbm, w3))):
        tall = src.shape[0] // PIECES
        group = []
        for piece in range(PIECES):
            span = pl.ds(piece * tall, tall)
            load = pltpu.make_async_copy(src.at[span], dst.at[span], w_sem.at[index, piece])
            if index == 0:
                load.start()
            group.append(load)
        loads.append(group)

    normed = layer_norm(frames_ref[...].astype(jnp.float32), ngain_ref[...])
    rows[me, :, 0:dim] = normed.astype(jnp.bfloat16)
    diagonal = lax.broadcasted_iota(jnp.int32, (tok, tok), 0) == lax.broadcasted_iota(
        jnp.int32, (tok, tok), 1
    )
    own_ids = jnp.where(diagonal, idrow_ref[...].astype(jnp.float32), 0.0)
    id_column = jnp.sum(own_ids, axis=1, keepdims=True)
    rows[me, :, dim : dim + LANES] = jnp.broadcast_to(id_column, (tok, LANES)).astype(jnp.bfloat16)
    pl.semaphore_wait(barrier, n - 1)

    core, chip = me % 2, me // 2
    x, z, depth = chip % 2, chip // 2, n // 4
    partner = chip * 2 + (1 - core)
    beside = (z * 2 + 1 - x) * 2 + core
    deep = dim // PIECES
    sent = []

    def piece_copy(block, piece, slot, to):
        end = dim + LANES if piece == PIECES - 1 else (piece + 1) * deep
        spot = rows.at[block, :, piece * deep : end]
        return pltpu.make_async_remote_copy(
            src_ref=spot,
            dst_ref=spot,
            send_sem=g_send.at[slot],
            recv_sem=g_recv.at[block, piece],
            device_id={"row": to},
            device_id_type=MESH,
        )

    def go(block, piece, to, when=True):
        copy = piece_copy(block, piece, len(sent), to)
        sent.append((copy, when))
        if when is True:
            copy.start()
        else:
            pl.when(when)(copy.start)

    def arrive(block, piece):
        piece_copy(block, piece, 0, partner).wait_recv()

    hops = [(step, way) for step in range(1, depth) for way in (1, -1)]

    def inside(level):
        return jnp.logical_and(level >= 0, level < depth)

    def rail(level, side):
        return (level * 2 + side) * 2 + core

    def finish(piece):
        for step, way in hops:
            origin = z - way * step
            block = rail(origin, 1 - x)
            pl.when(inside(origin))(functools.partial(arrive, block, piece))
            go(block, piece, partner, inside(origin))
        for other in range(n // 2):
            arrive(other * 2 + 1 - core, piece)
        loads[0][piece].wait()

    cw = 512

    def product(piece, cols):
        span = slice(piece * deep, (piece + 1) * deep)
        return jnp.dot(
            rows[:, :, span].reshape(n * tok, deep), w1[span, cols], preferred_element_type=jnp.float32
        )

    for piece in range(PIECES):
        go(me, piece, beside)
        for way in (1, -1):
            go(me, piece, rail(z + way, x), inside(z + way))
        go(me, piece, partner)
    for piece in range(PIECES):
        arrive(beside, piece)
        go(beside, piece, partner)
        for step, way in hops:
            origin = z - way * step
            block = rail(origin, x)
            here = inside(origin)
            pl.when(here)(functools.partial(arrive, block, piece))
            if step < depth - 1:
                go(block, piece, rail(z + way, x), jnp.logical_and(here, inside(z + way)))
            go(block, piece, beside, here)
            go(block, piece, partner, here)
        if piece > 0:
            finish(piece - 1)
            if piece == 1:
                for load in loads[1] + loads[2]:
                    load.start()

            @pl.loop(0, width // cw)
            def _(step):
                cols = pl.ds(pl.multiple_of(step * cw, cw), cw)
                if piece == 1:
                    acc[:, cols] = product(0, cols)
                else:
                    acc[:, cols] += product(piece - 1, cols)

    finish(PIECES - 1)
    every_id = rows[:, :, dim : dim + LANES].reshape(n * tok, LANES).astype(jnp.float32)
    lane = lax.broadcasted_iota(jnp.int32, (n * tok, LANES), 1).astype(jnp.float32)
    onehot = jnp.where(every_id == lane, 1.0, 0.0)
    onehot_t[...] = jnp.transpose(onehot)[0:clips].astype(jnp.bfloat16)

    @pl.loop(0, width // cw)
    def _(step):
        cols = pl.ds(pl.multiple_of(step * cw, cw), cw)
        pre_act = acc[:, cols] + product(PIECES - 1, cols)
        hidden = 0.5 * pre_act * (1.0 + lax.erf(pre_act * 0.7071067811865476))
        summed = jnp.dot(
            onehot_t[...], hidden.astype(jnp.bfloat16), preferred_element_type=jnp.float32
        )
        ph[:, cols] = (summed / FRAMES).astype(jnp.bfloat16)

    for copy, when in sent:
        if when is True:
            copy.wait_send()
        else:
            pl.when(when)(copy.wait_send)
    for load in loads[1]:
        load.wait()
    own_hot = jnp.where(
        lax.broadcasted_iota(jnp.int32, (clips, tok), 0) == idrow_ref[...], 1.0, 0.0
    ).astype(jnp.bfloat16)

    def term(owner):
        cols = pl.ds(pl.multiple_of(owner * bw, LANES), bw)
        residual = jnp.dot(own_hot, frames_ref[:, cols], preferred_element_type=jnp.float32)
        return residual / FRAMES + jnp.dot(
            ph[...], w2[:, cols], preferred_element_type=jnp.float32
        )

    def give(step):
        owner = (me + 1 + step) % n
        return pltpu.make_async_remote_copy(
            src_ref=part.at[owner],
            dst_ref=landed.at[me],
            send_sem=r_send.at[step],
            recv_sem=r_recv.at[me],
            device_id={"row": owner},
            device_id_type=MESH,
        )

    @pl.loop(0, n - 1)
    def _(step):
        owner = (me + 1 + step) % n
        part[owner] = term(owner)

        @pl.when(step > 0)
        def _():
            give(step - 1).start()

    total = term(me)
    give(n - 2).start()
    for step in range(1, n):
        source = (me + n - step) % n
        pltpu.make_async_remote_copy(
            src_ref=part.at[source],
            dst_ref=landed.at[source],
            send_sem=r_send.at[0],
            recv_sem=r_recv.at[source],
            device_id={"row": source},
            device_id_type=MESH,
        ).wait_recv()
        total = total + landed[source]
    red[me] = total
    for step in range(n - 1):
        give(step).wait_send()
    sent = spread_blocks(red, a_send, a_recv, n, me)

    pooled = red[...]
    average = jnp.sum(jnp.sum(pooled, axis=0), axis=-1, keepdims=True) / dim
    centered = pooled - average[None]
    variance = jnp.sum(jnp.sum(centered * centered, axis=0), axis=-1, keepdims=True) / dim
    scale = lax.rsqrt(variance + epsilon)
    for block in range(n):
        cols = slice(block * bw, (block + 1) * bw)
        conn[:, cols] = ((red[block] - average) * scale * cgain_ref[:, cols]).astype(jnp.bfloat16)
    for load in loads[2]:
        load.wait()
    projected = jnp.dot(conn[...], w3[...], preferred_element_type=jnp.float32)
    for clip in range(clips):
        proj[clip] = projected[clip : clip + 1]
    arrived[pl.ds(me, 1)] = proj[pl.ds(me, 1)]
    for copy in sent:
        copy.wait_send()
    outs = []
    for step in range(1, n):
        owner = (me + step) % n
        copy = pltpu.make_async_remote_copy(
            src_ref=proj.at[owner],
            dst_ref=arrived.at[me],
            send_sem=o_send.at[step],
            recv_sem=o_recv.at[me],
            device_id={"row": owner},
            device_id_type=MESH,
        )
        copy.start()
        outs.append(copy)
    for step in range(1, n):
        source = (me + n - step) % n
        pltpu.make_async_remote_copy(
            src_ref=proj.at[source],
            dst_ref=arrived.at[source],
            send_sem=o_send.at[0],
            recv_sem=o_recv.at[source],
            device_id={"row": source},
            device_id_type=MESH,
        ).wait_recv()
    for block in range(n):
        out_ref[:, block * ew : (block + 1) * ew] = arrived[block].astype(jnp.bfloat16)
    for copy in outs:
        copy.wait_send()


def fused(frames_in, clip_ids, norm_gain, expand_weight, reduce_weight, conn_gain, conn_weight):
    n = lax.axis_size("row")
    tok, dim = frames_in.shape
    width, ew = expand_weight.shape[1], conn_weight.shape[1]
    bw = dim // n
    vmem, hbm = pl.BlockSpec(memory_space=pltpu.VMEM), pl.BlockSpec(memory_space=pl.ANY)
    dma = pltpu.SemaphoreType.DMA
    f32, bf16 = jnp.float32, jnp.bfloat16
    return pl.pallas_call(
        functools.partial(kernel, n),
        name="vision_block",
        out_shape=jax.ShapeDtypeStruct((1, n * ew), bf16),
        in_specs=[vmem, vmem, vmem, hbm, hbm, vmem, hbm],
        out_specs=vmem,
        scratch_shapes=[
            pltpu.VMEM((n, tok, dim + LANES), bf16),
            pltpu.VMEM((n * tok, width), f32),
            pltpu.VMEM((dim, width), bf16),
            pltpu.VMEM((width, dim), bf16),
            pltpu.VMEM((dim, ew), bf16),
            pltpu.VMEM((n, n * tok), bf16),
            pltpu.VMEM((n, width), bf16),
            pltpu.VMEM((n, n, bw), f32),
            pltpu.VMEM((n, n, bw), f32),
            pltpu.VMEM((n, n, bw), f32),
            pltpu.VMEM((n, dim), bf16),
            pltpu.VMEM((n, 1, ew), f32),
            pltpu.VMEM((n, 1, ew), f32),
            dma((3, PIECES)),
            dma((2 * n * PIECES,)), dma((n, PIECES)), dma((n,)), dma((n,)),
            dma((n,)), dma((n,)), dma((n,)), dma((n,)),
        ],
        compiler_params=pltpu.CompilerParams(
            collective_id=0, has_side_effects=True, vmem_limit_bytes=60 * 1024 * 1024
        ),
    )(
        frames_in,
        clip_ids[None, :],
        norm_gain[None, :],
        expand_weight,
        reduce_weight,
        conn_gain[None, :],
        conn_weight,
    )


def local(frames_in, clip_ids, norm_gain, expand_weight, reduce_weight, conn_gain, conn_weight):
    n = lax.axis_size("row")
    tok, dim = frames_in.shape
    width, ew = expand_weight.shape[1], conn_weight.shape[1]
    fits = tok == FRAMES and n % 16 == 0 and n <= LANES and (n * tok) % LANES == 0
    even = dim % (n * LANES) == 0 and width % 512 == 0 and ew % LANES == 0
    form = fused if fits and even else plain
    return form(
        frames_in, clip_ids, norm_gain, expand_weight, reduce_weight, conn_gain, conn_weight
    )


def solution(mesh):
    in_specs = (
        P(("groups", "row"), None),
        P(("groups", "row")),
        P(),
        P(None, "row"),
        P("row", None),
        P(),
        P(None, "row"),
    )
    out_specs = P(("groups", "row"), None)
    return jax.shard_map(local, mesh=mesh, in_specs=in_specs, out_specs=out_specs, check_vma=False)
```
